32 devices in a mesh: param: 16 (over z, y, x), trace: 2 (over core).
Axes of the slice: x: 2, y: 2, z: 4, core: 2. Of those that a mesh axis runs over, the one named last changes fastest.
Arguments:
- grads: bfloat16 [8, 16777216], P('trace', 'param'), may hold values from -6 to 6
- signs: int32 [16777216], P('param'), may hold values 0 or 1
- kept: int32 [512], replicated, may hold values from 0 to 131071, as said below
Outputs:
- features: float32 [8, 65536], P(None, ('param', 'trace'))
The draws below stay inside these ranges and needn't reach their ends.
Inputs may be any that keep to these rules, and one draw needn't show every extreme that they name: `kept`: 512 distinct block numbers.
All inputs are finite; a program needn't handle non-finite values. No bound on the sum of `signs` on one device may be relied on, other than what follows from the above.
Results may differ from the reference program's by a relative error of at most 0.0003.
Values sent between devices are 32-bit elements; how exact they have to be, the bound alone decides.
A program may use at most 192 MiB of HBM per device.

```python
import jax
import jax.numpy as jnp
from jax import lax

D = 4096
BLOCK = 128
KEEP = 512
TRACES = 8
LENGTH = 16777216
N_PARAM = 16


def draw_kept(key, part):
    all_blocks = D * D // BLOCK
    key_level = jax.random.fold_in(key, 11)
    key_jitter = jax.random.fold_in(key, 23)
    positions = jnp.arange(all_blocks, dtype=jnp.int32)
    levels = jax.random.randint(key_level, (64,), 0, 4, dtype=jnp.int32)
    level_here = levels[positions // (all_blocks // 64)]
    jitter = jax.random.randint(key_jitter, (all_blocks,), 0, 1024, dtype=jnp.int32)
    scores = (jitter + 256 * level_here) * all_blocks + positions
    edges = (positions == 0) | (positions == all_blocks - 1)
    scores = jnp.where(edges, 2 ** 30 + positions, scores)
    _, chosen = lax.top_k(scores, KEEP)
    return chosen.astype(jnp.int32)


def set_ends(entries, rng, least, high):
    spot = [jax.random.randint(jax.random.fold_in(rng, axis), (), 0, length) for axis, length in enumerate(entries.shape)]
    longest = entries.shape.index(max(entries.shape))
    neighbour = spot[:longest] + [(spot[longest] + 1) % entries.shape[longest]] + spot[longest + 1:]
    return entries.at[tuple(spot)].set(least).at[tuple(neighbour)].set(high)


def block_levels(key, dims, shards, low, top_value):
    def one(axis_at, blocks):
        heights = jax.random.uniform(jax.random.fold_in(jax.random.fold_in(key, 6), axis_at), (blocks,), jnp.float32, low / len(shards), top_value / len(shards))
        return jnp.repeat(jnp.exp(heights), dims[axis_at] // blocks).reshape((-1,) + (1,) * (len(dims) - axis_at - 1))

    loudness = one(*shards[0])
    for cut in shards[1:]:
        loudness = loudness * one(*cut)
    return loudness


def gaussian(key, shape, scale, reach, pieces=(), kind=jnp.bfloat16):
    factor_of = block_levels(key, shape, pieces, -0.22, 0.18) if pieces else 1.0
    result = jax.random.normal(key, shape, jnp.float32) * scale * factor_of
    return jnp.minimum(jnp.maximum(result, -reach), reach).astype(kind)


def setup_inputs(seed: int = 0) -> dict:
    key_list = jax.random.split(jax.random.key(seed), 4)
    grads = gaussian(key_list[0], (TRACES, LENGTH), 1.0, 6.0, ((0, 2), (1, 16)))
    signs = set_ends((jax.random.randint(key_list[1], (LENGTH,), 0, 2) < 1).astype(jnp.int32), jax.random.fold_in(key_list[1], 1), 0, 1)
    kept = draw_kept(jax.random.fold_in(key_list[3], 71), 0)
    return {"grads": grads, "signs": signs, "kept": kept}


def parity_signs(row_values, col_values, bit_count):
    intersection = row_values[:, None] & col_values[None, :]
    parity = jnp.zeros(intersection.shape, jnp.int32)
    for bit_number in range(bit_count):
        parity = parity + ((intersection >> bit_number) & 1)
    return 1 - 2 * (parity % 2)


def reference(grads, signs, kept):
    length = D * D
    local_size = length // N_PARAM
    left_size = 2 ** ((local_size.bit_length() - 1) // 2)
    right_size = local_size // left_size
    left_table = parity_signs(jnp.arange(left_size, dtype=jnp.int32), jnp.arange(left_size, dtype=jnp.int32), left_size.bit_length()).astype(jnp.float32)
    right_table = parity_signs(jnp.arange(right_size, dtype=jnp.int32), jnp.arange(right_size, dtype=jnp.int32), right_size.bit_length()).astype(jnp.float32)
    blocks_dev = local_size // BLOCK
    region = (kept // blocks_dev).astype(jnp.int32)
    within = (kept % blocks_dev).astype(jnp.int32)
    mixing = parity_signs(region, jnp.arange(N_PARAM, dtype=jnp.int32), N_PARAM.bit_length()).astype(jnp.float32)

    def one_trace(trace_row):
        signed = jnp.where(signs == 1, trace_row, -trace_row).astype(jnp.float32).reshape(N_PARAM, left_size, right_size)
        half_done = jnp.einsum('ij,ajk->aik', left_table, signed, precision=lax.Precision.HIGHEST)
        whole = jnp.einsum('aik,kl->ail', half_done, right_table, precision=lax.Precision.HIGHEST)
        picked = whole.reshape(N_PARAM, blocks_dev, BLOCK)[:, within, :]
        mixed = jnp.einsum('fa,afc->fc', mixing, picked, precision=lax.Precision.HIGHEST)
        return (mixed / D).reshape(KEEP * BLOCK)

    return lax.map(one_trace, grads)
```

```python
import functools

import jax
import jax.numpy as jnp
from jax import lax
from jax.experimental import pallas as pl
from jax.experimental.pallas import tpu as pltpu
from jax.sharding import PartitionSpec as P

D = 4096
BLOCK = 128
SUB = 8


def parity(value):
    for shift in (16, 8, 4, 2, 1):
        value = value ^ (value >> shift)
    return value & 1


def sign_of(value):
    return (1 - 2 * parity(value)).astype(jnp.float32).astype(jnp.bfloat16)


def partial_kernel(kept_ref, x_ref, s_ref, o_ref, low_ref, wide_ref):
    step = pl.program_id(0)
    rows = s_ref.shape[0]
    traces = x_ref.shape[0] // rows
    kept = kept_ref[...]

    @pl.when(step == 0)
    def _():
        lane = lax.broadcasted_iota(jnp.int32, kept.shape, 1)
        for k in range(SUB):
            low_ref[:, k * BLOCK:(k + 1) * BLOCK] = sign_of(kept & (lane + k * BLOCK))

    upper = lax.axis_index("param") * pl.num_programs(0) + step
    high = sign_of(kept & (upper * (SUB * BLOCK)))
    table = low_ref[...] * jnp.concatenate([high] * SUB, axis=1)
    wide_ref[...] = x_ref[...].astype(jnp.float32)
    sign = (2 * s_ref[...] - 1).astype(jnp.float32)
    signed = jnp.concatenate(
        [(wide_ref[pl.ds(t, rows, stride=traces), :] * sign).astype(jnp.bfloat16) for t in range(traces)],
        axis=1,
    )
    term = jnp.dot(table, signed, preferred_element_type=jnp.float32)

    @pl.when(step == 0)
    def _():
        o_ref[...] = term

    @pl.when(step > 0)
    def _():
        o_ref[...] += term


def partial_sums(grads, signs, kept):
    traces, local_size = grads.shape
    keep = kept.shape[0]
    blocks = local_size // BLOCK
    rows = SUB * BLOCK
    x = grads.reshape(traces, blocks, BLOCK).transpose(1, 0, 2).reshape(blocks * traces, BLOCK)
    s = signs.reshape(blocks, BLOCK)
    kept_wide = jnp.broadcast_to(kept[:, None], (keep, BLOCK))
    return pl.pallas_call(
        partial_kernel,
        out_shape=jax.ShapeDtypeStruct((keep, traces * BLOCK), jnp.float32),
        grid=(blocks // rows,),
        in_specs=[
            pl.BlockSpec((keep, BLOCK), lambda i: (0, 0)),
            pl.BlockSpec((rows * traces, BLOCK), lambda i: (i, 0)),
            pl.BlockSpec((rows, BLOCK), lambda i: (i, 0)),
        ],
        out_specs=pl.BlockSpec((keep, traces * BLOCK), lambda i: (0, 0)),
        scratch_shapes=[
            pltpu.VMEM((keep, rows), jnp.bfloat16),
            pltpu.VMEM((rows * traces, BLOCK), jnp.float32),
        ],
        compiler_params=pltpu.CompilerParams(
            dimension_semantics=("arbitrary",), vmem_limit_bytes=60 << 20
        ),
    )(kept_wide, x, s)


def lane_table():
    index = jnp.arange(BLOCK, dtype=jnp.int32)
    return (1 - 2 * parity(index[:, None] & index[None, :])).astype(jnp.float32) / D


def per_device(grads, signs, kept):
    sums = partial_sums(grads, signs, kept)
    mine = lax.psum_scatter(sums, "param", scatter_dimension=0, tiled=True)
    both = lax.all_to_all(mine, "trace", split_axis=0, concat_axis=1, tiled=True)
    here = both.shape[0]
    split = both.reshape(here, -1, BLOCK)
    done = jnp.einsum("ftl,lc->tfc", split, lane_table(), precision=lax.Precision.HIGHEST)
    return done.reshape(-1, here * BLOCK)


def solution(mesh):
    placed = (P("trace", "param"), P("param"), P())
    return jax.shard_map(
        per_device,
        mesh=mesh,
        in_specs=placed,
        out_specs=P(None, ("param", "trace")),
        check_vma=False,
    )
```

```python
import functools

import jax
import jax.numpy as jnp
from jax import lax
from jax.experimental import pallas as pl
from jax.experimental.pallas import tpu as pltpu
from jax.sharding import PartitionSpec as P

D = 4096
BLOCK = 128
SUB = 8


def parity(value):
    for shift in (16, 8, 4, 2, 1):
        value = value ^ (value >> shift)
    return value & 1


def sign_of(value):
    return (1 - 2 * parity(value)).astype(jnp.float32).astype(jnp.bfloat16)


def partial_kernel(kept_ref, x_ref, s_ref, o_ref, low_ref, wide_ref):
    step = pl.program_id(0)
    rows = s_ref.shape[0]
    traces = x_ref.shape[0] // rows
    kept = kept_ref[...]

    @pl.when(step == 0)
    def _():
        lane = lax.broadcasted_iota(jnp.int32, kept.shape, 1)
        for k in range(SUB):
            low_ref[:, k * BLOCK:(k + 1) * BLOCK] = sign_of(kept & (lane + k * BLOCK))

    upper = lax.axis_index("param") * pl.num_programs(0) + step
    high = sign_of(kept & (upper * (SUB * BLOCK)))
    table = low_ref[...] * jnp.concatenate([high] * SUB, axis=1)
    wide_ref[...] = x_ref[...].astype(jnp.float32)
    sign = (2 * s_ref[...] - 1).astype(jnp.float32)
    signed = jnp.concatenate(
        [(wide_ref[pl.ds(t, rows, stride=traces), :] * sign).astype(jnp.bfloat16) for t in range(traces)],
        axis=1,
    )
    term = jnp.dot(table, signed, preferred_element_type=jnp.float32)

    @pl.when(step == 0)
    def _():
        o_ref[...] = term

    @pl.when(step > 0)
    def _():
        o_ref[...] += term


def partial_sums(grads, signs, kept):
    traces, local_size = grads.shape
    keep = kept.shape[0]
    blocks = local_size // BLOCK
    rows = SUB * BLOCK
    x = grads.reshape(traces, blocks, BLOCK).transpose(1, 0, 2).reshape(blocks * traces, BLOCK)
    s = signs.reshape(blocks, BLOCK)
    kept_wide = jnp.broadcast_to(kept[:, None], (keep, BLOCK))
    return pl.pallas_call(
        partial_kernel,
        out_shape=jax.ShapeDtypeStruct((keep, traces * BLOCK), jnp.float32),
        grid=(blocks // rows,),
        in_specs=[
            pl.BlockSpec((keep, BLOCK), lambda i: (0, 0)),
            pl.BlockSpec((rows * traces, BLOCK), lambda i: (i, 0)),
            pl.BlockSpec((rows, BLOCK), lambda i: (i, 0)),
        ],
        out_specs=pl.BlockSpec((keep, traces * BLOCK), lambda i: (0, 0)),
        scratch_shapes=[
            pltpu.VMEM((keep, rows), jnp.bfloat16),
            pltpu.VMEM((rows * traces, BLOCK), jnp.float32),
        ],
        compiler_params=pltpu.CompilerParams(
            dimension_semantics=("arbitrary",), vmem_limit_bytes=60 << 20
        ),
    )(kept_wide, x, s)


def cut_of(groups):
    bits = groups.bit_length() - 1
    minor = bits // 3
    return 2 ** (bits - 2 * minor), 2 ** minor, 2 ** minor


def parts_of(width):
    unit = width // 4
    return (
        (0, 2 * unit, (2, 1, 0)),
        (2 * unit, unit, (1, 0, 2)),
        (3 * unit, unit, (0, 2, 1)),
    )


def at_axis(ref, axis, index):
    return ref.at[(slice(None),) * axis + (index,)]


def combine_kernel(cut, parts, plan, sums_ref, o_ref, final_ref, other_ref, send_sem, recv_sem, *buffers):
    own = lax.axis_index("param")
    core = lax.axis_index("trace")
    spans = (cut[1] * cut[2], cut[2], 1)
    place = tuple((own // spans[d]) % cut[d] for d in range(3))

    def peer(d, offset):
        there = (place[d] + offset) % cut[d]
        return there, own + (there - place[d]) * spans[d]

    barrier = pltpu.get_barrier_semaphore()
    count = 0
    for d in range(3):
        for offset in range(1, cut[d]):
            pl.semaphore_signal(
                barrier, inc=1, device_id={"param": peer(d, offset)[1]}, device_id_type=pl.DeviceIdType.MESH
            )
            count += 1
    pl.semaphore_signal(barrier, inc=1, device_id={"trace": 1 - core}, device_id_type=pl.DeviceIdType.MESH)
    pl.semaphore_wait(barrier, count + 1)

    lanes = [pl.ds(low, width) for low, width, _ in parts]
    held = [sums_ref.at[:, :, :, :, lanes[n]] for n in range(len(parts))]
    flying = {}
    sent = []

    def launch(n, stage):
        d, axis, slots, result, first = plan[n][stage]
        copies = []
        for offset in range(1, cut[d]):
            there, device = peer(d, offset)
            copy = pltpu.make_async_remote_copy(
                src_ref=at_axis(held[n], axis, there),
                dst_ref=buffers[slots].at[offset - 1],
                send_sem=send_sem.at[first + offset - 1],
                recv_sem=recv_sem.at[first + offset - 1],
                device_id={"param": device},
                device_id_type=pl.DeviceIdType.MESH,
            )
            copy.start()
            copies.append(copy)
        flying[n, stage] = copies
        sent.extend(copies)

    for n in range(len(parts)):
        launch(n, 0)
    for stage in range(3):
        for n in range(len(parts)):
            d, axis, slots, result, first = plan[n][stage]
            total = at_axis(held[n], axis, place[d])[...]
            for offset in range(1, cut[d]):
                flying[n, stage][offset - 1].wait_recv()
                total = total + buffers[slots][offset - 1]
            if stage < 2:
                buffers[result][...] = total
                held[n] = buffers[result]
                launch(n, stage + 1)
            else:
                final_ref[:, lanes[n]] = total

    rows = final_ref.shape[0] // 2
    here = other_ref.shape[0]
    whole = here == 2 * rows
    swap = pltpu.make_async_remote_copy(
        src_ref=final_ref if whole else final_ref.at[pl.ds((1 - core) * rows, rows)],
        dst_ref=other_ref,
        send_sem=send_sem.at[send_sem.shape[0] - 1],
        recv_sem=recv_sem.at[recv_sem.shape[0] - 1],
        device_id={"trace": 1 - core},
        device_id_type=pl.DeviceIdType.MESH,
    )
    swap.start()
    mine = jnp.where(core == 0, final_ref[0:rows, :], final_ref[rows:2 * rows, :])
    swap.wait_recv()
    if whole:
        theirs = jnp.where(core == 0, other_ref[0:rows, :], other_ref[rows:2 * rows, :])
    else:
        theirs = other_ref[...]
    both = (jnp.where(core == 0, mine, theirs), jnp.where(core == 0, theirs, mine))
    local = final_ref.shape[1] // BLOCK
    for half in range(2):
        for t in range(local):
            o_ref[pl.ds(half * local + t, rows, stride=2 * local), :] = both[half][:, t * BLOCK:(t + 1) * BLOCK]
    index = lax.broadcasted_iota(jnp.int32, (BLOCK, BLOCK), 0) & lax.broadcasted_iota(jnp.int32, (BLOCK, BLOCK), 1)
    table = (1 - 2 * parity(index)).astype(jnp.float32) * (1.0 / D)
    o_ref[...] = jnp.dot(
        o_ref[...], table, precision=lax.Precision.HIGHEST, preferred_element_type=jnp.float32
    )
    for copy in sent:
        copy.wait_send()
    swap.wait_send()


def combine(sums, groups):
    keep, width = sums.shape
    cut = cut_of(groups)
    rows = keep // groups
    parts = parts_of(width)
    buffers, plan, first = [], [], 0
    for _, lanes, order in parts:
        left = [0, 1, 2]
        stages = []
        for d in order:
            axis = left.index(d)
            left.remove(d)
            rest = tuple(cut[k] for k in left)
            buffers.append(pltpu.VMEM((max(cut[d] - 1, 1), *rest, rows, lanes), jnp.float32))
            buffers.append(pltpu.VMEM((*rest, rows, lanes), jnp.float32))
            stages.append((d, axis, len(buffers) - 2, len(buffers) - 1, first))
            first += cut[d] - 1
        plan.append(stages)
    half = rows // 2
    out = pl.pallas_call(
        functools.partial(combine_kernel, cut, parts, plan),
        out_shape=jax.ShapeDtypeStruct((half * 2 * width // BLOCK, BLOCK), jnp.float32),
        in_specs=[pl.BlockSpec(memory_space=pltpu.VMEM)],
        out_specs=pl.BlockSpec(memory_space=pltpu.VMEM),
        scratch_shapes=[
            pltpu.VMEM((rows, width), jnp.float32),
            pltpu.VMEM((half if half % 8 == 0 else rows, width), jnp.float32),
            pltpu.SemaphoreType.DMA((first + 1,)),
            pltpu.SemaphoreType.DMA((first + 1,)),
            *buffers,
        ],
        compiler_params=pltpu.CompilerParams(
            collective_id=0, has_side_effects=True, vmem_limit_bytes=32 << 20
        ),
    )(sums.reshape(*cut, rows, width))
    return out.reshape(half, -1, BLOCK).transpose(1, 0, 2).reshape(-1, half * BLOCK)


def per_device(grads, signs, kept):
    return combine(partial_sums(grads, signs, kept), lax.axis_size("param"))


def solution(mesh):
    placed = (P("trace", "param"), P("param"), P())
    return jax.shard_map(
        per_device,
        mesh=mesh,
        in_specs=placed,
        out_specs=P(None, ("param", "trace")),
        check_vma=False,
    )
```

```python
import functools

import jax
import jax.numpy as jnp
from jax import lax
from jax.experimental import pallas as pl
from jax.experimental.pallas import tpu as pltpu
from jax.sharding import PartitionSpec as P

D = 4096
BLOCK = 128
SUB = 8


def parity(value):
    for shift in (16, 8, 4, 2, 1):
        value = value ^ (value >> shift)
    return value & 1


def sign_of(value):
    return (1 - 2 * parity(value)).astype(jnp.float32).astype(jnp.bfloat16)


def cut_of(groups):
    bits = groups.bit_length() - 1
    minor = bits // 3
    return 2 ** (bits - 2 * minor), 2 ** minor, 2 ** minor


def parts_of(width):
    unit = width // 4
    return (
        (0, 2 * unit, (2, 1, 0)),
        (2 * unit, unit, (1, 0, 2)),
        (3 * unit, unit, (0, 2, 1)),
    )


def at_axis(ref, axis, index):
    return ref.at[(slice(None),) * axis + (index,)]


def partial_sums(kept_ref, x_hbm, s_hbm, x_ref, s_ref, x_sem, s_sem, wide_ref, low_ref, sums_ref):
    steps, rows = s_ref.shape[0], s_ref.shape[1]
    traces = x_ref.shape[1] // rows
    groups = kept_ref.shape[0]
    lane = lax.broadcasted_iota(jnp.int32, (BLOCK, BLOCK), 1)
    kept = jnp.concatenate(
        [jnp.broadcast_to(kept_ref[n:n + 1, :], (BLOCK, BLOCK)).T for n in range(groups)], axis=0
    )
    lane = jnp.concatenate([lane] * groups, axis=0)
    for k in range(SUB):
        low_ref[:, k * BLOCK:(k + 1) * BLOCK] = sign_of(kept & (lane + k * BLOCK))
    base = lax.axis_index("param") * steps

    def term(step):
        pltpu.make_async_copy(x_hbm.at[step], x_ref.at[step], x_sem.at[step]).wait()
        pltpu.make_async_copy(s_hbm.at[step], s_ref.at[step], s_sem.at[step]).wait()
        high = sign_of(kept & ((base + step) * (SUB * BLOCK)))
        table = low_ref[...] * jnp.concatenate([high] * SUB, axis=1)
        wide_ref[...] = x_ref[step].astype(jnp.float32)
        sign = (2 * s_ref[step] - 1).astype(jnp.float32)
        signed = jnp.concatenate(
            [(wide_ref[pl.ds(t, rows, stride=traces), :] * sign).astype(jnp.bfloat16) for t in range(traces)],
            axis=1,
        )
        return jnp.dot(table, signed, preferred_element_type=jnp.float32).reshape(sums_ref.shape)

    sums_ref[...] = term(0)

    @pl.loop(1, steps)
    def _(step):
        sums_ref[...] += term(step)


def fused_kernel(
    cut, parts, plan, kept_ref, x_hbm, s_hbm, o_ref, x_ref, s_ref, x_sem, s_sem, wide_ref, low_ref, sums_ref,
    final_ref, other_ref, send_sem, recv_sem, *buffers
):
    @pl.loop(0, s_ref.shape[0])
    def _(step):
        pltpu.make_async_copy(x_hbm.at[step], x_ref.at[step], x_sem.at[step]).start()
        pltpu.make_async_copy(s_hbm.at[step], s_ref.at[step], s_sem.at[step]).start()

    own = lax.axis_index("param")
    core = lax.axis_index("trace")
    spans = (cut[1] * cut[2], cut[2], 1)
    place = tuple((own // spans[d]) % cut[d] for d in range(3))

    def peer(d, offset):
        there = (place[d] + offset) % cut[d]
        return there, own + (there - place[d]) * spans[d]

    barrier = pltpu.get_barrier_semaphore()
    count = 0
    for d in range(3):
        for offset in range(1, cut[d]):
            pl.semaphore_signal(
                barrier, inc=1, device_id={"param": peer(d, offset)[1]}, device_id_type=pl.DeviceIdType.MESH
            )
            count += 1
    pl.semaphore_signal(barrier, inc=1, device_id={"trace": 1 - core}, device_id_type=pl.DeviceIdType.MESH)
    partial_sums(kept_ref, x_hbm, s_hbm, x_ref, s_ref, x_sem, s_sem, wide_ref, low_ref, sums_ref)
    pl.semaphore_wait(barrier, count + 1)

    lanes = [pl.ds(low, width) for low, width, _ in parts]
    held = [sums_ref.at[:, :, :, :, lanes[n]] for n in range(len(parts))]
    flying = {}
    sent = []

    def launch(n, stage):
        d, axis, slots, result, first = plan[n][stage]
        copies = []
        for offset in range(1, cut[d]):
            there, device = peer(d, offset)
            copy = pltpu.make_async_remote_copy(
                src_ref=at_axis(held[n], axis, there),
                dst_ref=buffers[slots].at[offset - 1],
                send_sem=send_sem.at[first + offset - 1],
                recv_sem=recv_sem.at[first + offset - 1],
                device_id={"param": device},
                device_id_type=pl.DeviceIdType.MESH,
            )
            copy.start()
            copies.append(copy)
        flying[n, stage] = copies
        sent.extend(copies)

    for n in range(len(parts)):
        launch(n, 0)
    for stage in range(3):
        for n in range(len(parts)):
            d, axis, slots, result, first = plan[n][stage]
            total = at_axis(held[n], axis, place[d])[...]
            for offset in range(1, cut[d]):
                flying[n, stage][offset - 1].wait_recv()
                total = total + buffers[slots][offset - 1]
            if stage < 2:
                buffers[result][...] = total
                held[n] = buffers[result]
                launch(n, stage + 1)
            else:
                final_ref[:, lanes[n]] = total

    rows = final_ref.shape[0] // 2
    here = other_ref.shape[0]
    whole = here == 2 * rows
    swap = pltpu.make_async_remote_copy(
        src_ref=final_ref if whole else final_ref.at[pl.ds((1 - core) * rows, rows)],
        dst_ref=other_ref,
        send_sem=send_sem.at[send_sem.shape[0] - 1],
        recv_sem=recv_sem.at[recv_sem.shape[0] - 1],
        device_id={"trace": 1 - core},
        device_id_type=pl.DeviceIdType.MESH,
    )
    swap.start()
    mine = jnp.where(core == 0, final_ref[0:rows, :], final_ref[rows:2 * rows, :])
    swap.wait_recv()
    if whole:
        theirs = jnp.where(core == 0, other_ref[0:rows, :], other_ref[rows:2 * rows, :])
    else:
        theirs = other_ref[...]
    both = (jnp.where(core == 0, mine, theirs), jnp.where(core == 0, theirs, mine))
    local = final_ref.shape[1] // BLOCK
    for half in range(2):
        for t in range(local):
            o_ref[pl.ds(half * local + t, rows, stride=2 * local), :] = both[half][:, t * BLOCK:(t + 1) * BLOCK]
    index = lax.broadcasted_iota(jnp.int32, (BLOCK, BLOCK), 0) & lax.broadcasted_iota(jnp.int32, (BLOCK, BLOCK), 1)
    table = (1 - 2 * parity(index)).astype(jnp.float32) * (1.0 / D)
    o_ref[...] = jnp.dot(
        o_ref[...], table, precision=lax.Precision.HIGHEST, preferred_element_type=jnp.float32
    )
    for copy in sent:
        copy.wait_send()
    swap.wait_send()


def per_device(grads, signs, kept):
    traces, local_size = grads.shape
    groups = lax.axis_size("param")
    keep, width = kept.shape[0], traces * BLOCK
    blocks = local_size // BLOCK
    chunk = SUB * BLOCK
    steps = blocks // chunk
    x = grads.reshape(traces, blocks, BLOCK).transpose(1, 0, 2).reshape(steps, chunk * traces, BLOCK)
    s = signs.reshape(steps, chunk, BLOCK)
    cut = cut_of(groups)
    rows = keep // groups
    parts = parts_of(width)
    buffers, plan, first = [], [], 0
    for _, lanes, order in parts:
        left = [0, 1, 2]
        stages = []
        for d in order:
            axis = left.index(d)
            left.remove(d)
            rest = tuple(cut[k] for k in left)
            buffers.append(pltpu.VMEM((max(cut[d] - 1, 1), *rest, rows, lanes), jnp.float32))
            buffers.append(pltpu.VMEM((*rest, rows, lanes), jnp.float32))
            stages.append((d, axis, len(buffers) - 2, len(buffers) - 1, first))
            first += cut[d] - 1
        plan.append(stages)
    half = rows // 2
    out = pl.pallas_call(
        functools.partial(fused_kernel, cut, parts, plan),
        out_shape=jax.ShapeDtypeStruct((half * 2 * width // BLOCK, BLOCK), jnp.float32),
        in_specs=[
            pl.BlockSpec(memory_space=pltpu.VMEM),
            pl.BlockSpec(memory_space=pl.ANY),
            pl.BlockSpec(memory_space=pl.ANY),
        ],
        out_specs=pl.BlockSpec(memory_space=pltpu.VMEM),
        scratch_shapes=[
            pltpu.VMEM(x.shape, x.dtype),
            pltpu.VMEM(s.shape, s.dtype),
            pltpu.SemaphoreType.DMA((steps,)),
            pltpu.SemaphoreType.DMA((steps,)),
            pltpu.VMEM(x.shape[1:], jnp.float32),
            pltpu.VMEM((keep, chunk), jnp.bfloat16),
            pltpu.VMEM((*cut, rows, width), jnp.float32),
            pltpu.VMEM((rows, width), jnp.float32),
            pltpu.VMEM((half if half % 8 == 0 else rows, width), jnp.float32),
            pltpu.SemaphoreType.DMA((first + 1,)),
            pltpu.SemaphoreType.DMA((first + 1,)),
            *buffers,
        ],
        compiler_params=pltpu.CompilerParams(
            collective_id=0, has_side_effects=True, vmem_limit_bytes=60 << 20
        ),
    )(kept.reshape(-1, BLOCK), x, s)
    return out.reshape(half, -1, BLOCK).transpose(1, 0, 2).reshape(-1, half * BLOCK)


def solution(mesh):
    placed = (P("trace", "param"), P("param"), P())
    return jax.shard_map(
        per_device,
        mesh=mesh,
        in_specs=placed,
        out_specs=P(None, ("param", "trace")),
        check_vma=False,
    )
```

```python
import functools

import jax
import jax.numpy as jnp
from jax import lax
from jax.experimental import pallas as pl
from jax.experimental.pallas import tpu as pltpu
from jax.sharding import PartitionSpec as P

D = 4096
BLOCK = 128
SUB = 8


def parity(value):
    for shift in (16, 8, 4, 2, 1):
        value = value ^ (value >> shift)
    return value & 1


def sign_of(value):
    return (1 - 2 * parity(value)).astype(jnp.float32).astype(jnp.bfloat16)


def cut_of(groups):
    bits = groups.bit_length() - 1
    minor = bits // 3
    return 2 ** (bits - 2 * minor), 2 ** minor, 2 ** minor


def parts_of(width):
    unit = width // 4
    return (
        (0, 2 * unit, (2, 1, 0)),
        (2 * unit, unit, (1, 0, 2)),
        (3 * unit, unit, (0, 2, 1)),
    )


def at_axis(ref, axis, index):
    return ref.at[(slice(None),) * axis + (index,)]


def partial_sums(kept_ref, x_hbm, s_hbm, x_ref, s_ref, x_sem, s_sem, wide_refs, ready_refs, low_ref, sums_ref):
    steps, rows = s_ref.shape[0], s_ref.shape[1]
    traces = x_ref.shape[1] // rows
    groups = kept_ref.shape[0]
    lane = lax.broadcasted_iota(jnp.int32, (BLOCK, BLOCK), 1)
    kept = jnp.concatenate(
        [jnp.broadcast_to(kept_ref[n:n + 1, :], (BLOCK, BLOCK)).T for n in range(groups)], axis=0
    )
    lane = jnp.concatenate([lane] * groups, axis=0)
    for k in range(SUB):
        low_ref[:, k * BLOCK:(k + 1) * BLOCK] = sign_of(kept & (lane + k * BLOCK))
    base = lax.axis_index("param") * steps

    def prepare(step, slot):
        pltpu.make_async_copy(x_hbm.at[step], x_ref.at[step], x_sem.at[step]).wait()
        pltpu.make_async_copy(s_hbm.at[step], s_ref.at[step], s_sem.at[step]).wait()
        wide_refs[slot][...] = x_ref[step].astype(jnp.float32)
        sign = (2 * s_ref[step] - 1).astype(jnp.float32)
        for t in range(traces):
            ready_refs[slot][:, t * BLOCK:(t + 1) * BLOCK] = (
                wide_refs[slot][pl.ds(t, rows, stride=traces), :] * sign
            ).astype(jnp.bfloat16)

    def term(step, slot):
        high = sign_of(kept & ((base + step) * (SUB * BLOCK)))
        table = low_ref[...] * jnp.concatenate([high] * SUB, axis=1)
        found = jnp.dot(table, ready_refs[slot][...], preferred_element_type=jnp.float32)
        return found.reshape(sums_ref.shape)

    sums_ref[...] = jnp.zeros_like(sums_ref)
    prepare(0, 0)

    @pl.loop(0, steps // 2 - 1)
    def _(pair):
        prepare(2 * pair + 1, 1)
        sums_ref[...] += term(2 * pair, 0)
        prepare(2 * pair + 2, 0)
        sums_ref[...] += term(2 * pair + 1, 1)

    prepare(steps - 1, 1)
    sums_ref[...] += term(steps - 2, 0)
    sums_ref[...] += term(steps - 1, 1)


def fused_kernel(
    cut, parts, plan, kept_ref, x_hbm, s_hbm, o_ref, x_ref, s_ref, x_sem, s_sem, wide_a, wide_b,
    ready_a, ready_b, low_ref, sums_ref, final_ref, other_ref, send_sem, recv_sem, *buffers
):
    @pl.loop(0, s_ref.shape[0])
    def _(step):
        pltpu.make_async_copy(x_hbm.at[step], x_ref.at[step], x_sem.at[step]).start()
        pltpu.make_async_copy(s_hbm.at[step], s_ref.at[step], s_sem.at[step]).start()

    own = lax.axis_index("param")
    core = lax.axis_index("trace")
    spans = (cut[1] * cut[2], cut[2], 1)
    place = tuple((own // spans[d]) % cut[d] for d in range(3))

    def peer(d, offset):
        there = (place[d] + offset) % cut[d]
        return there, own + (there - place[d]) * spans[d]

    barrier = pltpu.get_barrier_semaphore()
    count = 0
    for d in range(3):
        for offset in range(1, cut[d]):
            pl.semaphore_signal(
                barrier, inc=1, device_id={"param": peer(d, offset)[1]}, device_id_type=pl.DeviceIdType.MESH
            )
            count += 1
    pl.semaphore_signal(barrier, inc=1, device_id={"trace": 1 - core}, device_id_type=pl.DeviceIdType.MESH)
    partial_sums(
        kept_ref, x_hbm, s_hbm, x_ref, s_ref, x_sem, s_sem, (wide_a, wide_b), (ready_a, ready_b), low_ref, sums_ref
    )
    pl.semaphore_wait(barrier, count + 1)

    lanes = [pl.ds(low, width) for low, width, _ in parts]
    held = [sums_ref.at[:, :, :, :, lanes[n]] for n in range(len(parts))]
    flying = {}
    sent = []

    def launch(n, stage):
        d, axis, slots, result, first = plan[n][stage]
        copies = []
        for offset in range(1, cut[d]):
            there, device = peer(d, offset)
            copy = pltpu.make_async_remote_copy(
                src_ref=at_axis(held[n], axis, there),
                dst_ref=buffers[slots].at[offset - 1],
                send_sem=send_sem.at[first + offset - 1],
                recv_sem=recv_sem.at[first + offset - 1],
                device_id={"param": device},
                device_id_type=pl.DeviceIdType.MESH,
            )
            copy.start()
            copies.append(copy)
        flying[n, stage] = copies
        sent.extend(copies)

    for n in range(len(parts)):
        launch(n, 0)
    for stage in range(3):
        for n in range(len(parts)):
            d, axis, slots, result, first = plan[n][stage]
            total = at_axis(held[n], axis, place[d])[...]
            for offset in range(1, cut[d]):
                flying[n, stage][offset - 1].wait_recv()
                total = total + buffers[slots][offset - 1]
            if stage < 2:
                buffers[result][...] = total
                held[n] = buffers[result]
                launch(n, stage + 1)
            else:
                final_ref[:, lanes[n]] = total

    rows = final_ref.shape[0] // 2
    here = other_ref.shape[0]
    whole = here == 2 * rows
    swap = pltpu.make_async_remote_copy(
        src_ref=final_ref if whole else final_ref.at[pl.ds((1 - core) * rows, rows)],
        dst_ref=other_ref,
        send_sem=send_sem.at[send_sem.shape[0] - 1],
        recv_sem=recv_sem.at[recv_sem.shape[0] - 1],
        device_id={"trace": 1 - core},
        device_id_type=pl.DeviceIdType.MESH,
    )
    swap.start()
    mine = jnp.where(core == 0, final_ref[0:rows, :], final_ref[rows:2 * rows, :])
    swap.wait_recv()
    if whole:
        theirs = jnp.where(core == 0, other_ref[0:rows, :], other_ref[rows:2 * rows, :])
    else:
        theirs = other_ref[...]
    both = (jnp.where(core == 0, mine, theirs), jnp.where(core == 0, theirs, mine))
    local = final_ref.shape[1] // BLOCK
    for half in range(2):
        for t in range(local):
            o_ref[pl.ds(half * local + t, rows, stride=2 * local), :] = both[half][:, t * BLOCK:(t + 1) * BLOCK]
    index = lax.broadcasted_iota(jnp.int32, (BLOCK, BLOCK), 0) & lax.broadcasted_iota(jnp.int32, (BLOCK, BLOCK), 1)
    table = (1 - 2 * parity(index)).astype(jnp.float32) * (1.0 / D)
    o_ref[...] = jnp.dot(
        o_ref[...], table, precision=lax.Precision.HIGHEST, preferred_element_type=jnp.float32
    )
    for copy in sent:
        copy.wait_send()
    swap.wait_send()


def per_device(grads, signs, kept):
    traces, local_size = grads.shape
    groups = lax.axis_size("param")
    keep, width = kept.shape[0], traces * BLOCK
    blocks = local_size // BLOCK
    chunk = SUB * BLOCK
    steps = blocks // chunk
    x = grads.reshape(traces, blocks, BLOCK).transpose(1, 0, 2).reshape(steps, chunk * traces, BLOCK)
    s = signs.reshape(steps, chunk, BLOCK)
    cut = cut_of(groups)
    rows = keep // groups
    parts = parts_of(width)
    buffers, plan, first = [], [], 0
    for _, lanes, order in parts:
        left = [0, 1, 2]
        stages = []
        for d in order:
            axis = left.index(d)
            left.remove(d)
            rest = tuple(cut[k] for k in left)
            buffers.append(pltpu.VMEM((max(cut[d] - 1, 1), *rest, rows, lanes), jnp.float32))
            buffers.append(pltpu.VMEM((*rest, rows, lanes), jnp.float32))
            stages.append((d, axis, len(buffers) - 2, len(buffers) - 1, first))
            first += cut[d] - 1
        plan.append(stages)
    half = rows // 2
    out = pl.pallas_call(
        functools.partial(fused_kernel, cut, parts, plan),
        out_shape=jax.ShapeDtypeStruct((half * 2 * width // BLOCK, BLOCK), jnp.float32),
        in_specs=[
            pl.BlockSpec(memory_space=pltpu.VMEM),
            pl.BlockSpec(memory_space=pl.ANY),
            pl.BlockSpec(memory_space=pl.ANY),
        ],
        out_specs=pl.BlockSpec(memory_space=pltpu.VMEM),
        scratch_shapes=[
            pltpu.VMEM(x.shape, x.dtype),
            pltpu.VMEM(s.shape, s.dtype),
            pltpu.SemaphoreType.DMA((steps,)),
            pltpu.SemaphoreType.DMA((steps,)),
            pltpu.VMEM(x.shape[1:], jnp.float32),
            pltpu.VMEM(x.shape[1:], jnp.float32),
            pltpu.VMEM((chunk, width), jnp.bfloat16),
            pltpu.VMEM((chunk, width), jnp.bfloat16),
            pltpu.VMEM((keep, chunk), jnp.bfloat16),
            pltpu.VMEM((*cut, rows, width), jnp.float32),
            pltpu.VMEM((rows, width), jnp.float32),
            pltpu.VMEM((half if half % 8 == 0 else rows, width), jnp.float32),
            pltpu.SemaphoreType.DMA((first + 1,)),
            pltpu.SemaphoreType.DMA((first + 1,)),
            *buffers,
        ],
        compiler_params=pltpu.CompilerParams(
            collective_id=0, has_side_effects=True, vmem_limit_bytes=60 << 20
        ),
    )(kept.reshape(-1, BLOCK), x, s)
    return out.reshape(half, -1, BLOCK).transpose(1, 0, 2).reshape(-1, half * BLOCK)


def solution(mesh):
    placed = (P("trace", "param"), P("param"), P())
    return jax.shard_map(
        per_device,
        mesh=mesh,
        in_specs=placed,
        out_specs=P(None, ("param", "trace")),
        check_vma=False,
    )
```

```python
import functools

import jax
import jax.numpy as jnp
from jax import lax
from jax.experimental import pallas as pl
from jax.experimental.pallas import tpu as pltpu
from jax.sharding import PartitionSpec as P

D = 4096
BLOCK = 128
SUB = 8


def parity(value):
    for shift in (16, 8, 4, 2, 1):
        value = value ^ (value >> shift)
    return value & 1


def sign_of(value):
    return (1 - 2 * parity(value)).astype(jnp.float32).astype(jnp.bfloat16)


def cut_of(groups):
    bits = groups.bit_length() - 1
    minor = bits // 3
    return 2 ** (bits - 2 * minor), 2 ** minor, 2 ** minor


def parts_of(width):
    unit = width // 4
    return (
        (0, 2 * unit, (2, 1, 0)),
        (2 * unit, unit, (1, 0, 2)),
        (3 * unit, unit, (0, 2, 1)),
    )


def at_axis(ref, axis, index):
    return ref.at[(slice(None),) * axis + (index,)]


def partial_sums(kept_ref, x_hbm, s_hbm, x_ref, s_ref, x_sem, s_sem, wide_ref, rest_ref, low_ref, early_ref, late_ref, send_early):
    steps, rows = s_ref.shape[0], s_ref.shape[1]
    traces = x_ref.shape[1] // rows
    groups = kept_ref.shape[0]
    lane = lax.broadcasted_iota(jnp.int32, (BLOCK, BLOCK), 1)
    kept = jnp.concatenate(
        [jnp.broadcast_to(kept_ref[n:n + 1, :], (BLOCK, BLOCK)).T for n in range(groups)], axis=0
    )
    lane = jnp.concatenate([lane] * groups, axis=0)
    for k in range(SUB):
        low_ref[:, k * BLOCK:(k + 1) * BLOCK] = sign_of(kept & (lane + k * BLOCK))
    base = lax.axis_index("param") * steps

    half = traces // 2

    def table_of(step):
        high = sign_of(kept & ((base + step) * (SUB * BLOCK)))
        return low_ref[...] * jnp.concatenate([high] * SUB, axis=1)

    early_ref[...] = jnp.zeros_like(early_ref)
    late_ref[...] = jnp.zeros_like(late_ref)

    @pl.loop(0, steps)
    def _(step):
        pltpu.make_async_copy(x_hbm.at[step], x_ref.at[step], x_sem.at[step]).wait()
        pltpu.make_async_copy(s_hbm.at[step], s_ref.at[step], s_sem.at[step]).wait()
        wide_ref[...] = x_ref[step].astype(jnp.float32)
        sign = (2 * s_ref[step] - 1).astype(jnp.float32)
        signed = [
            (wide_ref[pl.ds(t, rows, stride=traces), :] * sign).astype(jnp.bfloat16) for t in range(traces)
        ]
        for t in range(half, traces):
            rest_ref[step, :, (t - half) * BLOCK:(t - half + 1) * BLOCK] = signed[t]
        early_ref[...] += jnp.dot(
            table_of(step), jnp.concatenate(signed[:half], axis=1), preferred_element_type=jnp.float32
        ).reshape(early_ref.shape)

    send_early()

    @pl.loop(0, steps)
    def _(step):
        late_ref[...] += jnp.dot(
            table_of(step), rest_ref[step], preferred_element_type=jnp.float32
        ).reshape(late_ref.shape)


def fused_kernel(
    cut, parts, plan, kept_ref, x_hbm, s_hbm, o_ref, x_ref, s_ref, x_sem, s_sem, wide_ref, rest_ref, low_ref,
    early_ref, late_ref, final_ref, other_ref, send_sem, recv_sem, *buffers
):
    @pl.loop(0, s_ref.shape[0])
    def _(step):
        pltpu.make_async_copy(x_hbm.at[step], x_ref.at[step], x_sem.at[step]).start()
        pltpu.make_async_copy(s_hbm.at[step], s_ref.at[step], s_sem.at[step]).start()

    own = lax.axis_index("param")
    core = lax.axis_index("trace")
    spans = (cut[1] * cut[2], cut[2], 1)
    place = tuple((own // spans[d]) % cut[d] for d in range(3))

    def peer(d, offset):
        there = (place[d] + offset) % cut[d]
        return there, own + (there - place[d]) * spans[d]

    barrier = pltpu.get_barrier_semaphore()
    count = 0
    for d in range(3):
        for offset in range(1, cut[d]):
            pl.semaphore_signal(
                barrier, inc=1, device_id={"param": peer(d, offset)[1]}, device_id_type=pl.DeviceIdType.MESH
            )
            count += 1
    pl.semaphore_signal(barrier, inc=1, device_id={"trace": 1 - core}, device_id_type=pl.DeviceIdType.MESH)
    lanes = [pl.ds(low, width) for low, width, _ in parts]
    unit = parts[1][1]
    held = [early_ref, late_ref.at[:, :, :, :, pl.ds(0, unit)], late_ref.at[:, :, :, :, pl.ds(unit, unit)]]
    flying = {}
    sent = []

    def launch(n, stage):
        d, axis, slots, result, first = plan[n][stage]
        copies = []
        for offset in range(1, cut[d]):
            there, device = peer(d, offset)
            copy = pltpu.make_async_remote_copy(
                src_ref=at_axis(held[n], axis, there),
                dst_ref=buffers[slots].at[offset - 1],
                send_sem=send_sem.at[first + offset - 1],
                recv_sem=recv_sem.at[first + offset - 1],
                device_id={"param": device},
                device_id_type=pl.DeviceIdType.MESH,
            )
            copy.start()
            copies.append(copy)
        flying[n, stage] = copies
        sent.extend(copies)

    def send_early():
        pl.semaphore_wait(barrier, count + 1)
        launch(0, 0)

    partial_sums(
        kept_ref, x_hbm, s_hbm, x_ref, s_ref, x_sem, s_sem, wide_ref, rest_ref, low_ref, early_ref, late_ref, send_early
    )
    launch(1, 0)
    launch(2, 0)
    for stage in range(3):
        for n in range(len(parts)):
            d, axis, slots, result, first = plan[n][stage]
            total = at_axis(held[n], axis, place[d])[...]
            for offset in range(1, cut[d]):
                flying[n, stage][offset - 1].wait_recv()
                total = total + buffers[slots][offset - 1]
            if stage < 2:
                buffers[result][...] = total
                held[n] = buffers[result]
                launch(n, stage + 1)
            else:
                final_ref[:, lanes[n]] = total

    rows = final_ref.shape[0] // 2
    here = other_ref.shape[0]
    whole = here == 2 * rows
    swap = pltpu.make_async_remote_copy(
        src_ref=final_ref if whole else final_ref.at[pl.ds((1 - core) * rows, rows)],
        dst_ref=other_ref,
        send_sem=send_sem.at[send_sem.shape[0] - 1],
        recv_sem=recv_sem.at[recv_sem.shape[0] - 1],
        device_id={"trace": 1 - core},
        device_id_type=pl.DeviceIdType.MESH,
    )
    swap.start()
    mine = jnp.where(core == 0, final_ref[0:rows, :], final_ref[rows:2 * rows, :])
    swap.wait_recv()
    if whole:
        theirs = jnp.where(core == 0, other_ref[0:rows, :], other_ref[rows:2 * rows, :])
    else:
        theirs = other_ref[...]
    both = (jnp.where(core == 0, mine, theirs), jnp.where(core == 0, theirs, mine))
    local = final_ref.shape[1] // BLOCK
    for half in range(2):
        for t in range(local):
            o_ref[pl.ds(half * local + t, rows, stride=2 * local), :] = both[half][:, t * BLOCK:(t + 1) * BLOCK]
    index = lax.broadcasted_iota(jnp.int32, (BLOCK, BLOCK), 0) & lax.broadcasted_iota(jnp.int32, (BLOCK, BLOCK), 1)
    table = (1 - 2 * parity(index)).astype(jnp.float32) * (1.0 / D)
    o_ref[...] = jnp.dot(
        o_ref[...], table, precision=lax.Precision.HIGHEST, preferred_element_type=jnp.float32
    )
    for copy in sent:
        copy.wait_send()
    swap.wait_send()


def per_device(grads, signs, kept):
    traces, local_size = grads.shape
    groups = lax.axis_size("param")
    keep, width = kept.shape[0], traces * BLOCK
    blocks = local_size // BLOCK
    chunk = SUB * BLOCK
    steps = blocks // chunk
    x = grads.reshape(traces, blocks, BLOCK).transpose(1, 0, 2).reshape(steps, chunk * traces, BLOCK)
    s = signs.reshape(steps, chunk, BLOCK)
    cut = cut_of(groups)
    rows = keep // groups
    parts = parts_of(width)
    buffers, plan, first = [], [], 0
    for _, lanes, order in parts:
        left = [0, 1, 2]
        stages = []
        for d in order:
            axis = left.index(d)
            left.remove(d)
            rest = tuple(cut[k] for k in left)
            buffers.append(pltpu.VMEM((max(cut[d] - 1, 1), *rest, rows, lanes), jnp.float32))
            buffers.append(pltpu.VMEM((*rest, rows, lanes), jnp.float32))
            stages.append((d, axis, len(buffers) - 2, len(buffers) - 1, first))
            first += cut[d] - 1
        plan.append(stages)
    half = rows // 2
    out = pl.pallas_call(
        functools.partial(fused_kernel, cut, parts, plan),
        out_shape=jax.ShapeDtypeStruct((half * 2 * width // BLOCK, BLOCK), jnp.float32),
        in_specs=[
            pl.BlockSpec(memory_space=pltpu.VMEM),
            pl.BlockSpec(memory_space=pl.ANY),
            pl.BlockSpec(memory_space=pl.ANY),
        ],
        out_specs=pl.BlockSpec(memory_space=pltpu.VMEM),
        scratch_shapes=[
            pltpu.VMEM(x.shape, x.dtype),
            pltpu.VMEM(s.shape, s.dtype),
            pltpu.SemaphoreType.DMA((steps,)),
            pltpu.SemaphoreType.DMA((steps,)),
            pltpu.VMEM(x.shape[1:], jnp.float32),
            pltpu.VMEM((steps, chunk, width // 2), jnp.bfloat16),
            pltpu.VMEM((keep, chunk), jnp.bfloat16),
            pltpu.VMEM((*cut, rows, width // 2), jnp.float32),
            pltpu.VMEM((*cut, rows, width // 2), jnp.float32),
            pltpu.VMEM((rows, width), jnp.float32),
            pltpu.VMEM((half if half % 8 == 0 else rows, width), jnp.float32),
            pltpu.SemaphoreType.DMA((first + 1,)),
            pltpu.SemaphoreType.DMA((first + 1,)),
            *buffers,
        ],
        compiler_params=pltpu.CompilerParams(
            collective_id=0, has_side_effects=True, vmem_limit_bytes=60 << 20
        ),
    )(kept.reshape(-1, BLOCK), x, s)
    return out.reshape(half, -1, BLOCK).transpose(1, 0, 2).reshape(-1, half * BLOCK)


def solution(mesh):
    placed = (P("trace", "param"), P("param"), P())
    return jax.shard_map(
        per_device,
        mesh=mesh,
        in_specs=placed,
        out_specs=P(None, ("param", "trace")),
        check_vma=False,
    )
```
